256 devices in a mesh: bulk: 16 (over y, z_hi), col: 16 (over x, z_lo, core).
Axes of the slice: x: 4, y: 4, z: 8 (z_hi: 4, z_lo: 2; z = z_hi * 2 + z_lo), core: 2. Of those that a mesh axis runs over, the one named last changes fastest.
Arguments:
- sigma_m: bfloat16 [16384, 16384], P('bulk', 'col'), may hold values from -0.046875 to 0.046875
- sigma_n: bfloat16 [16384, 16384], P('bulk', 'col'), may hold values from -0.046875 to 0.046875
- coeffs: bfloat16 [24576, 16384], P('bulk', 'col'), may hold values from -0.0390625 to 0.0390625
- s_half: bfloat16 [24576, 512], P(('bulk', 'col')), may hold values from -6 to 6
Outputs:
- updated: float32 [24576, 512], P(('bulk', 'col'))
The draws below stay inside these ranges and needn't reach their ends.
All inputs are finite; a program needn't handle non-finite values.
Results may differ from the reference program's by a relative error of at most 0.0051.
Values may be sent and summed in bfloat16 or wider, within the bound.
A program may use at most 128 MiB of HBM per device.

```python
import jax
import jax.numpy as jnp
from jax import lax

BASIS = 24576
STATES = 16384
PANEL = 512


def block_scale(own_key, dims, split, low, largest):
    factor_of = 1.0
    for axis_at, parts in split:
        heights = jax.random.uniform(jax.random.fold_in(jax.random.fold_in(own_key, 6), axis_at), (parts,), jnp.float32, low / len(split), largest / len(split))
        factor_of = factor_of * jnp.repeat(jnp.exp(heights), dims[axis_at] // parts).reshape((-1,) + (1,) * (len(dims) - 1 - axis_at))
    return factor_of


def noise(key, extent, spread, bound, pieces=(), dtype=jnp.bfloat16):
    result = spread * jax.random.normal(key, extent, jnp.float32)
    if pieces:
        result = result * block_scale(key, extent, pieces, -0.22, 0.18)
    return jnp.clip(result, -bound, bound).astype(dtype)


def setup_inputs(seed: int = 0) -> dict:
    seeds = jax.random.split(jax.random.key(seed), 5)
    sigma_m = noise(seeds[0], (STATES, STATES), STATES ** -0.5, 0.046875, ((0, 16), (1, 16)))
    sigma_n = noise(seeds[1], (STATES, STATES), STATES ** -0.5, 0.046875, ((0, 16), (1, 16)))
    coeffs = noise(seeds[2], (BASIS, STATES), BASIS ** -0.5, 0.0390625, ((0, 16), (1, 16)))
    s_half = noise(seeds[3], (BASIS, PANEL), 1.0, 6.0, ((0, 256),))
    return {"sigma_m": sigma_m, "sigma_n": sigma_n, "coeffs": coeffs, "s_half": s_half}


def reference(sigma_m, sigma_n, coeffs, s_half):
    mixed = (0.5 * (sigma_m.astype(jnp.float32) + sigma_n.astype(jnp.float32))).astype(jnp.bfloat16)
    projected = lax.dot_general(coeffs, s_half, (((0,), (0,)), ((), ())), preferred_element_type=jnp.float32).astype(jnp.bfloat16)
    direct = jnp.dot(mixed, projected, preferred_element_type=jnp.float32)
    flipped = lax.dot_general(mixed, projected, (((0,), (0,)), ((), ())), preferred_element_type=jnp.float32)
    rotated = (0.5 * (direct + flipped)).astype(jnp.bfloat16)
    return jnp.dot(coeffs, rotated, preferred_element_type=jnp.float32)
```

```python
import jax
import jax.numpy as jnp
from jax import lax
from jax.experimental import pallas as pl
from jax.experimental.pallas import tpu as pltpu
from jax.sharding import PartitionSpec as P

BF, F32 = jnp.bfloat16, jnp.float32
GROUPS, LANES = 4, 128
CHUNKS = 2
SLOTS = ((0, 2, 3, 1), (0, 1, 2, 3))


def place(colour, v):
    if colour == 0:
        return ((v + 1) // 2) % 2, v // 2
    return v // 2, v % 2


def partners(colour, v):
    near, far = v + 1 - 2 * (v % 2), 3 - v
    return (near, far) if colour == 0 else (far, near)


def dot(a, b, da, db):
    return lax.dot_general(a, b, (((da,), (db,)), ((), ())), preferred_element_type=F32)


def kernel(sm_hbm, sn_hbm, co_hbm, s_ref, o_ref, bufs, sems):
    b, c = lax.axis_index("bulk"), lax.axis_index("col")
    y, h = b // 4, b % 4
    x, l, k = c // 4, (c // 2) % 2, c % 2
    hl, hk = h // 2, h % 2

    def dev(y=y, h=h, x=x, l=l, k=k):
        return {"bulk": y * 4 + h, "col": x * 4 + l * 2 + k}

    flipped = {"bulk": c, "col": b}
    B, S = bufs, sems
    pending = []

    loads = [
        pltpu.make_async_copy(src, dst, S["load"].at[i])
        for i, (src, dst) in enumerate(
            ((sm_hbm, B["sm"]), (sn_hbm, B["sn"]), (co_hbm, B["co"]))
        )
    ]
    for ld in loads:
        ld.start()

    bar = pltpu.get_barrier_semaphore()
    shifts = [(dx, dl) for dx in range(4) for dl in range(2) if dx or dl]
    peers = [dev(x=(x + dx) % 4, l=(l + dl) % 2) for dx, dl in shifts]
    greeted = peers + [dev(k=1 - k), dev(y=y + 1 - 2 * (y % 2)), dev(y=3 - y)]
    greeted += [dev(h=(h + j) % 4) for j in (1, 2, 3)]
    greeted += [flipped]
    for to in greeted:
        pl.semaphore_signal(bar, inc=1, device_id=to)

    for p in range(CHUNKS):
        B["sg"][p, x, l, k] = s_ref[:, p * 256 : (p + 1) * 256]

    pl.semaphore_wait(bar, len(greeted))

    def send(src, dst, sem, at, to):
        cp = pltpu.make_async_remote_copy(
            src_ref=src,
            dst_ref=dst,
            send_sem=S[sem].at[(0, *at)],
            recv_sem=S[sem].at[(1, *at)],
            device_id=to,
        )
        cp.start()
        pending.append(cp)
        return cp

    own_s = [B["sg"].at[p, x, l, k] for p in range(CHUNKS)]
    arrive = [
        [send(own_s[p], own_s[p], "a", (p, j), to) for j, to in enumerate(peers)]
        for p in range(CHUNKS)
    ]
    across = [
        [send(own_s[p], own_s[p], "ac", (p, 7), dev(k=1 - k))] for p in range(CHUNKS)
    ]

    loads[0].wait()
    loads[1].wait()

    def mix(i, _):
        r = pl.ds(pl.multiple_of(i * 64, 64), 64)
        total = B["sm"][r, :].astype(F32) + B["sn"][r, :].astype(F32)
        B["mx"][r, :] = (0.5 * total).astype(BF)
        return 0

    lax.fori_loop(0, 16, mix, 0)
    loads[2].wait()

    def split_rows(name, p, value, rows):
        for i in range(2):
            part = value[:, i * LANES : (i + 1) * LANES]
            B[name][2 * p + i] = part.reshape(4, 2, 2, rows, LANES)

    def joined(name, p):
        return jnp.concatenate(
            [B[name][2 * p + i].reshape(-1, LANES) for i in range(2)], axis=1
        )

    def bulk_sum_1(n, g):
        half, _ = place(g % 2, y)
        B[n + "_s1"][g] = B[n][g, pl.ds(2 * (1 - half), 2)].astype(BF)
        to = dev(y=partners(g % 2, y)[0])
        return send(B[n + "_s1"].at[g], B[n + "_r1"].at[g], n + "_1", (g,), to)

    def bulk_sum_2(n, g, cp):
        cp.wait_recv()
        half, quart = place(g % 2, y)
        f, r1 = B[n], B[n + "_r1"]
        other = f[g, 2 * half + 1 - quart] + r1[g, 1 - quart].astype(F32)
        B[n + "_s2"][g] = other.astype(BF)
        to = dev(y=partners(g % 2, y)[1])
        cp = send(B[n + "_s2"].at[g], B[n + "_r2"].at[g], n + "_2", (g,), to)
        f[g, 2 * half + quart] = f[g, 2 * half + quart] + r1[g, quart].astype(F32)
        return cp

    def bulk_sum_3(n, g, cp):
        cp.wait_recv()
        half, quart = place(g % 2, y)
        total = B[n][g, 2 * half + quart] + B[n + "_r2"][g].astype(F32)
        B[n + "_s3"][g] = total.astype(B[n + "_s3"].dtype)
        cps = []
        for j in (1, 2, 3):
            to = (h + j) % 4
            cps.append(
                send(
                    B[n + "_s3"].at[g, to // 2, to % 2],
                    B[n + "_r3"].at[g, j - 1],
                    n + "_3",
                    (g, j - 1),
                    dev(h=to),
                )
            )
        own = B[n][g, 2 * half + quart, hl, hk]
        B[n + "_own"][g] = own + B[n + "_r2"][g, hl, hk].astype(F32)
        return cps

    def bulk_sum_end(n, g, cps):
        for cp in cps:
            cp.wait_recv()
        r3 = B[n + "_r3"]
        total = B[n + "_own"][g] + r3[g, 0].astype(F32)
        return total + (r3[g, 1].astype(F32) + r3[g, 2].astype(F32))

    def bulk_gather_1(n, g):
        half, quart = place(g % 2, y)
        piece = B[n].at[g, 2 * half + quart, hl, hk]
        return [
            send(piece, piece, n + "_g1", (g, j - 1), dev(h=(h + j) % 4))
            for j in (1, 2, 3)
        ]

    def bulk_gather_2(n, g, cps):
        for cp in cps:
            cp.wait_recv()
        half, quart = place(g % 2, y)
        piece = B[n].at[g, 2 * half + quart]
        return send(piece, piece, n + "_g2", (g,), dev(y=partners(g % 2, y)[1]))

    def bulk_gather_3(n, g, cp):
        cp.wait_recv()
        half, _ = place(g % 2, y)
        piece = B[n].at[g, pl.ds(2 * half, 2)]
        return send(piece, piece, n + "_g3", (g,), dev(y=partners(g % 2, y)[0]))

    def col_sum_1(n, g):
        return send(
            B[n].at[g, :, :, 1 - k], B[n + "_r1"].at[g], n + "_1", (g,), dev(k=1 - k)
        )

    def col_sum_2(n, g, cp):
        cp.wait_recv()
        half, _ = place(g % 2, x)
        f, r1, away = B[n], B[n + "_r1"], pl.ds(2 * (1 - half), 2)
        out = f[g, away, :, k] + r1[g, away]
        B[n + "_s2"][g] = out.astype(B[n + "_s2"].dtype)
        to = dev(x=partners(g % 2, x)[0])
        cp = send(B[n + "_s2"].at[g], B[n + "_r2"].at[g], n + "_2", (g,), to)
        here = pl.ds(2 * half, 2)
        B[n + "_h"][g] = f[g, here, :, k] + r1[g, here]
        return cp

    def col_sum_3(n, g, cp):
        cp.wait_recv()
        _, quart = place(g % 2, x)
        f, r2 = B[n + "_h"], B[n + "_r2"]
        out = f[g, 1 - quart] + r2[g, 1 - quart].astype(F32)
        B[n + "_s3"][g] = out.astype(B[n + "_s3"].dtype)
        to = dev(x=partners(g % 2, x)[1])
        cp = send(B[n + "_s3"].at[g], B[n + "_r3"].at[g], n + "_3", (g,), to)
        B[n + "_q"][g] = f[g, quart] + r2[g, quart].astype(F32)
        return cp

    def col_sum_4(n, g, cp):
        cp.wait_recv()
        f, r3 = B[n + "_q"], B[n + "_r3"]
        out = f[g, 1 - l] + r3[g, 1 - l].astype(F32)
        B[n + "_s4"][g] = out.astype(B[n + "_s4"].dtype)
        return send(
            B[n + "_s4"].at[g], B[n + "_r4"].at[g], n + "_4", (g,), dev(l=1 - l)
        )

    def col_sum_end(n, g, cp):
        cp.wait_recv()
        f, r3 = B[n + "_q"], B[n + "_r3"]
        return f[g, l] + r3[g, l].astype(F32) + B[n + "_r4"][g].astype(F32)

    def flip(src, dst, sem, g):
        cp = pltpu.make_async_remote_copy(
            src_ref=src,
            dst_ref=dst,
            send_sem=S[sem].at[0, g],
            recv_sem=S[sem].at[1, g],
            device_id=flipped,
        )

        @pl.when(b != c)
        def _():
            cp.start()

        @pl.when(b == c)
        def _():
            dst[...] = src[...]

        return cp

    def flip_wait(cp):
        @pl.when(b != c)
        def _():
            cp.wait()

    def col_gather_1(n, g, cp):
        flip_wait(cp)
        half, quart = place(g % 2, x)
        piece = B[n].at[g, 2 * half + quart, l, k]
        return send(piece, piece, n + "_g1", (g,), dev(l=1 - l))

    def col_gather_2(n, g, cp):
        cp.wait_recv()
        half, quart = place(g % 2, x)
        piece = B[n].at[g, 2 * half + quart, :, k]
        return send(piece, piece, n + "_g2", (g,), dev(x=partners(g % 2, x)[1]))

    def col_gather_3(n, g, cp):
        cp.wait_recv()
        half, _ = place(g % 2, x)
        piece = B[n].at[g, pl.ds(2 * half, 2), :, k]
        return send(piece, piece, n + "_g3", (g,), dev(x=partners(g % 2, x)[0]))

    def col_gather_4(n, g, cp):
        cp.wait_recv()
        piece = B[n].at[g, :, :, k]
        return send(piece, piece, n + "_g4", (g,), dev(k=1 - k))

    groups = range(GROUPS)
    of_chunk = [(2 * p, 2 * p + 1) for p in range(CHUNKS)]

    cp = {}
    for p in range(CHUNKS):
        for j, (dx, dl) in enumerate(shifts):
            arrive[p][j].wait_recv()
            block = B["sg"].at[p, (x - dx + 4) % 4, (l - dl + 2) % 2, k]
            across[p].append(send(block, block, "ac", (p, j), dev(k=1 - k)))
        for one in across[p]:
            one.wait_recv()
        rows = B["sg"][p].reshape(-1, 2 * LANES)
        split_rows("fp", p, dot(B["co"][...], rows, 0, 0), 64)
        for g in of_chunk[p]:
            cp[g] = bulk_sum_1("fp", g)
    for g in groups:
        cp[g] = bulk_sum_2("fp", g, cp[g])
    for g in groups:
        cp[g] = bulk_sum_3("fp", g, cp[g])
    near, far = {}, {}
    for g in groups:
        half, quart = place(g % 2, y)
        at = (g, 2 * half + quart, hl, hk)
        B["pc"][at] = bulk_sum_end("fp", g, cp[g]).astype(BF)
        near[g] = bulk_gather_1("pc", g)
        far[g] = flip(B["pc"].at[at], B["pr"].at[at], "pr_t", g)

    for g in groups:
        far[g] = col_gather_1("pr", g, far[g])
    for g in groups:
        near[g] = bulk_gather_2("pc", g, near[g])
    for g in groups:
        far[g] = col_gather_2("pr", g, far[g])
    for g in groups:
        near[g] = bulk_gather_3("pc", g, near[g])
    for g in groups:
        far[g] = col_gather_3("pr", g, far[g])
    for g in groups:
        far[g] = col_gather_4("pr", g, far[g])
    row, col = {}, {}
    for p in range(CHUNKS):
        for g in of_chunk[p]:
            near[g].wait_recv()
        split_rows("fr", p, dot(B["mx"][...], joined("pc", p), 1, 0), 64)
        for g in of_chunk[p]:
            row[g] = col_sum_1("fr", g)
        for g in of_chunk[p]:
            far[g].wait_recv()
        split_rows("fc", p, dot(B["mx"][...], joined("pr", p), 0, 0), 64)
        for g in of_chunk[p]:
            col[g] = bulk_sum_1("fc", g)

    for g in groups:
        row[g] = col_sum_2("fr", g, row[g])
    for g in groups:
        col[g] = bulk_sum_2("fc", g, col[g])
    for g in groups:
        row[g] = col_sum_3("fr", g, row[g])
    for g in groups:
        col[g] = bulk_sum_3("fc", g, col[g])
    for g in groups:
        row[g] = col_sum_4("fr", g, row[g])
    for g in groups:
        B["fr_t"][g] = col_sum_end("fr", g, row[g])
        row[g] = flip(B["fr_t"].at[g], B["fr_u"].at[g], "fr_t", g)
    for g in groups:
        total = bulk_sum_end("fc", g, col[g])
        flip_wait(row[g])
        half, quart = place(g % 2, y)
        rotated = (0.5 * (total + B["fr_u"][g])).astype(BF)
        B["ro"][g, 2 * half + quart, hl, hk] = rotated
        near[g] = bulk_gather_1("ro", g)
    for g in groups:
        near[g] = bulk_gather_2("ro", g, near[g])
    for g in groups:
        near[g] = bulk_gather_3("ro", g, near[g])

    for p in range(CHUNKS):
        for g in of_chunk[p]:
            near[g].wait_recv()
        value = dot(B["co"][...], joined("ro", p), 1, 0)
        for g in of_chunk[p]:
            i = g % 2
            part = value[:, i * LANES : (i + 1) * LANES].reshape(4, 2, 2, 96, LANES)
            for v in range(4):
                B["fu"][g, SLOTS[i][v]] = part[v]
            row[g] = col_sum_1("fu", g)
    for g in groups:
        row[g] = col_sum_2("fu", g, row[g])
    for g in groups:
        row[g] = col_sum_3("fu", g, row[g])
    for g in groups:
        row[g] = col_sum_4("fu", g, row[g])
    for g in groups:
        o_ref[:, g * LANES : (g + 1) * LANES] = col_sum_end("fu", g, row[g])
    for one in pending:
        one.wait_send()


def scratch():
    V = pltpu.VMEM

    def bulk(n, z):
        return {
            n: V((GROUPS, 4, 2, 2, 64, LANES), F32),
            n + "_s1": V((GROUPS, 2, 2, 2, 64, LANES), BF),
            n + "_r1": V((GROUPS, 2, 2, 2, 64, LANES), BF),
            n + "_s2": V((GROUPS, 2, 2, 64, LANES), BF),
            n + "_r2": V((GROUPS, 2, 2, 64, LANES), BF),
            n + "_s3": V((GROUPS, 2, 2, 64, LANES), z),
            n + "_r3": V((GROUPS, 3, 64, LANES), z),
            n + "_own": V((GROUPS, 64, LANES), F32),
        }

    def col(n, rows, two, three, four):
        return {
            n: V((GROUPS, 4, 2, 2, rows, LANES), F32),
            n + "_r1": V((GROUPS, 4, 2, rows, LANES), F32),
            n + "_h": V((GROUPS, 2, 2, rows, LANES), F32),
            n + "_s2": V((GROUPS, 2, 2, rows, LANES), two),
            n + "_r2": V((GROUPS, 2, 2, rows, LANES), two),
            n + "_q": V((GROUPS, 2, rows, LANES), F32),
            n + "_s3": V((GROUPS, 2, rows, LANES), three),
            n + "_r3": V((GROUPS, 2, rows, LANES), three),
            n + "_s4": V((GROUPS, rows, LANES), four),
            n + "_r4": V((GROUPS, rows, LANES), four),
        }

    whole = (GROUPS, 4, 2, 2, 64, LANES)
    bufs = {
        "sm": V((1024, 1024), BF),
        "sn": V((1024, 1024), BF),
        "mx": V((1024, 1024), BF),
        "co": V((1536, 1024), BF),
        "sg": V((CHUNKS, 4, 2, 2, 96, 2 * LANES), BF),
        "pc": V(whole, BF),
        "pr": V(whole, BF),
        "ro": V(whole, BF),
        "fr_t": V((GROUPS, 64, LANES), F32),
        "fr_u": V((GROUPS, 64, LANES), F32),
        **bulk("fp", BF),
        **bulk("fc", BF),
        **col("fr", 64, F32, F32, F32),
        **col("fu", 96, BF, BF, BF),
    }
    D = pltpu.SemaphoreType.DMA
    sems = {"load": D((3,)), "a": D((2, CHUNKS, 7)), "ac": D((2, CHUNKS, 8))}
    for n in ("fp", "fc"):
        sems.update({n + "_1": D((2, GROUPS)), n + "_2": D((2, GROUPS))})
        sems[n + "_3"] = D((2, GROUPS, 3))
    for n in ("pc", "ro"):
        sems.update({n + "_g2": D((2, GROUPS)), n + "_g3": D((2, GROUPS))})
        sems[n + "_g1"] = D((2, GROUPS, 3))
    for i in range(1, 5):
        for n in ("fr_", "fu_", "pr_g"):
            sems[n + str(i)] = D((2, GROUPS))
    sems["pr_t"] = D((2, GROUPS))
    sems["fr_t"] = D((2, GROUPS))
    return bufs, sems


def shards(sigma_m, sigma_n, coeffs, s_half):
    bufs, sems = scratch()
    names, sem_names = list(bufs), list(sems)

    def body(*refs):
        rest = refs[5:]
        return kernel(
            *refs[:5],
            dict(zip(names, rest[: len(names)])),
            dict(zip(sem_names, rest[len(names) :])),
        )

    hbm, vmem = pl.BlockSpec(memory_space=pl.ANY), pl.BlockSpec(memory_space=pltpu.VMEM)
    return pl.pallas_call(
        body,
        out_shape=jax.ShapeDtypeStruct(s_half.shape, F32),
        in_specs=[hbm, hbm, hbm, vmem],
        out_specs=vmem,
        scratch_shapes=[*bufs.values(), *sems.values()],
        compiler_params=pltpu.CompilerParams(
            collective_id=0, has_side_effects=True, vmem_limit_bytes=60 << 20
        ),
        name="gw_update",
    )(sigma_m, sigma_n, coeffs, s_half)


def solution(mesh):
    in_specs = (P("bulk", "col"),) * 3 + (P(("bulk", "col"), None),)
    return jax.shard_map(
        shards,
        mesh=mesh,
        in_specs=in_specs,
        out_specs=P(("bulk", "col"), None),
        check_vma=False,
    )
```

```python
import jax
import jax.numpy as jnp
from jax import lax
from jax.experimental import pallas as pl
from jax.experimental.pallas import tpu as pltpu
from jax.sharding import PartitionSpec as P

BF, F32 = jnp.bfloat16, jnp.float32
GROUPS, LANES = 4, 128
CHUNKS = 2
SLOTS = ((0, 2, 3, 1), (0, 1, 2, 3))


def place(colour, v):
    if colour == 0:
        return ((v + 1) // 2) % 2, v // 2
    return v // 2, v % 2


def partners(colour, v):
    near, far = v + 1 - 2 * (v % 2), 3 - v
    return (near, far) if colour == 0 else (far, near)


def dot(a, b, da, db):
    return lax.dot_general(a, b, (((da,), (db,)), ((), ())), preferred_element_type=F32)


def kernel(sm_hbm, sn_hbm, co_hbm, s_ref, o_ref, bufs, sems):
    b, c = lax.axis_index("bulk"), lax.axis_index("col")
    y, h = b // 4, b % 4
    x, l, k = c // 4, (c // 2) % 2, c % 2
    hl, hk = h // 2, h % 2

    def dev(y=y, h=h, x=x, l=l, k=k):
        return {"bulk": y * 4 + h, "col": x * 4 + l * 2 + k}

    w = 2 * l + k
    v, u = (y - x + 4) % 4, (h - w + 4) % 4
    ul, uk = u // 2, u % 2

    flip_to = {"bulk": c, "col": ((x - y + 4) % 4) * 4 + (w - h + 4) % 4}
    flip_back = {"bulk": v * 4 + u, "col": b}

    fixed = (b == 0) & (c == 0)
    B, S = bufs, sems
    pending, pending_flips = [], []

    loads = [
        pltpu.make_async_copy(src, dst, S["load"].at[i])
        for i, (src, dst) in enumerate(
            ((sm_hbm, B["sm"]), (sn_hbm, B["sn"]), (co_hbm, B["co"]))
        )
    ]
    for ld in loads:
        ld.start()

    bar = pltpu.get_barrier_semaphore()
    shifts = [(dx, dl) for dx in range(4) for dl in range(2) if dx or dl]
    peers = [dev(x=(x + dx) % 4, l=(l + dl) % 2) for dx, dl in shifts]
    greeted = peers + [dev(k=1 - k), dev(y=y + 1 - 2 * (y % 2)), dev(y=3 - y)]
    greeted += [dev(h=(h + j) % 4) for j in (1, 2, 3)]
    greeted += [flip_to, flip_back]
    for to in greeted:
        pl.semaphore_signal(bar, inc=1, device_id=to)

    for p in range(CHUNKS):
        B["sg"][p, x, l, k] = s_ref[:, p * 256 : (p + 1) * 256]

    pl.semaphore_wait(bar, len(greeted))

    def send(src, dst, sem, at, to):
        cp = pltpu.make_async_remote_copy(
            src_ref=src,
            dst_ref=dst,
            send_sem=S[sem].at[(0, *at)],
            recv_sem=S[sem].at[(1, *at)],
            device_id=to,
        )
        cp.start()
        pending.append(cp)
        return cp

    own_s = [B["sg"].at[p, x, l, k] for p in range(CHUNKS)]
    arrive = [
        [send(own_s[p], own_s[p], "a", (p, j), to) for j, to in enumerate(peers)]
        for p in range(CHUNKS)
    ]
    across = [
        [send(own_s[p], own_s[p], "ac", (p, 7), dev(k=1 - k))] for p in range(CHUNKS)
    ]

    loads[0].wait()
    loads[1].wait()

    def mix(i, _):
        r = pl.ds(pl.multiple_of(i * 64, 64), 64)
        total = B["sm"][r, :].astype(F32) + B["sn"][r, :].astype(F32)
        B["mx"][r, :] = (0.5 * total).astype(BF)
        return 0

    lax.fori_loop(0, 16, mix, 0)
    loads[2].wait()

    def split_rows(name, p, value, rows):
        for i in range(2):
            part = value[:, i * LANES : (i + 1) * LANES]
            B[name][2 * p + i] = part.reshape(4, 2, 2, rows, LANES)

    def joined(name, p):
        return jnp.concatenate(
            [B[name][2 * p + i].reshape(-1, LANES) for i in range(2)], axis=1
        )

    def bulk_sum_1(n, g):
        half, _ = place(g % 2, y)
        B[n + "_s1"][g] = B[n][g, pl.ds(2 * (1 - half), 2)].astype(BF)
        to = dev(y=partners(g % 2, y)[0])
        return send(B[n + "_s1"].at[g], B[n + "_r1"].at[g], n + "_1", (g,), to)

    def bulk_sum_2(n, g, cp):
        cp.wait_recv()
        half, quart = place(g % 2, y)
        f, r1 = B[n], B[n + "_r1"]
        other = f[g, 2 * half + 1 - quart] + r1[g, 1 - quart].astype(F32)
        B[n + "_s2"][g] = other.astype(BF)
        to = dev(y=partners(g % 2, y)[1])
        cp = send(B[n + "_s2"].at[g], B[n + "_r2"].at[g], n + "_2", (g,), to)
        f[g, 2 * half + quart] = f[g, 2 * half + quart] + r1[g, quart].astype(F32)
        return cp

    def bulk_sum_3(n, g, cp):
        cp.wait_recv()
        half, quart = place(g % 2, y)
        total = B[n][g, 2 * half + quart] + B[n + "_r2"][g].astype(F32)
        B[n + "_s3"][g] = total.astype(B[n + "_s3"].dtype)
        cps = []
        for j in (1, 2, 3):
            to = (h + j) % 4
            cps.append(
                send(
                    B[n + "_s3"].at[g, to // 2, to % 2],
                    B[n + "_r3"].at[g, j - 1],
                    n + "_3",
                    (g, j - 1),
                    dev(h=to),
                )
            )
        own = B[n][g, 2 * half + quart, hl, hk]
        B[n + "_own"][g] = own + B[n + "_r2"][g, hl, hk].astype(F32)
        return cps

    def bulk_sum_end(n, g, cps):
        for cp in cps:
            cp.wait_recv()
        r3 = B[n + "_r3"]
        total = B[n + "_own"][g] + r3[g, 0].astype(F32)
        return total + (r3[g, 1].astype(F32) + r3[g, 2].astype(F32))

    def bulk_gather_1(n, g):
        half, quart = place(g % 2, y)
        piece = B[n].at[g, 2 * half + quart, hl, hk]
        first, second = partners(g % 2, y)
        z = {
            j: send(piece, piece, n + "_g1", (g, j - 1), dev(h=(h + j) % 4))
            for j in (1, 3, 2)
        }
        y2 = {0: send(piece, piece, n + "_g2", (g, 0), dev(y=second))}
        y1 = {0: send(piece, piece, n + "_g3", (g, 0), dev(y=first))}
        return z, y2, y1

    def bulk_gather_2(n, g, cps):
        z, y2, y1 = cps
        half, quart = place(g % 2, y)
        first, second = partners(g % 2, y)
        for j in (1, 3, 2):
            z[j].wait_recv()
            at = (h - j + 4) % 4
            piece = B[n].at[g, 2 * half + quart, at // 2, at % 2]
            y2[j] = send(piece, piece, n + "_g2", (g, j), dev(y=second))
            y1[j] = send(piece, piece, n + "_g3", (g, j), dev(y=first))

    def bulk_gather_3(n, g, cps, which):
        _, y2, y1 = cps
        half, quart = place(g % 2, y)
        first, _ = partners(g % 2, y)
        for j in which:
            y2[j].wait_recv()
            at = (h - j + 4) % 4
            piece = B[n].at[g, 2 * half + 1 - quart, at // 2, at % 2]
            y1[4 + j] = send(piece, piece, n + "_g3", (g, 4 + j), dev(y=first))

    def bulk_gather_end(cps):
        for j in range(8):
            cps[2][j].wait_recv()

    plain = (x, l, k, lambda at: at)
    turned = (v, ul, uk, lambda at: (y - at + 4) % 4)
    spot = {"fu": plain, "fr": turned}

    def col_sum_1(n, g):
        _, _, sk, _ = spot[n]
        return send(
            B[n].at[g, :, :, 1 - sk], B[n + "_r1"].at[g], n + "_1", (g,), dev(k=1 - k)
        )

    def col_sum_2(n, g, cp):
        cp.wait_recv()
        sx, _, sk, ring = spot[n]
        half, _ = place(g % 2, sx)
        f, r1, away = B[n], B[n + "_r1"], pl.ds(2 * (1 - half), 2)
        out = f[g, away, :, sk] + r1[g, away]
        B[n + "_s2"][g] = out.astype(B[n + "_s2"].dtype)
        to = dev(x=ring(partners(g % 2, sx)[0]))
        cp = send(B[n + "_s2"].at[g], B[n + "_r2"].at[g], n + "_2", (g,), to)
        here = pl.ds(2 * half, 2)
        B[n + "_h"][g] = f[g, here, :, sk] + r1[g, here]
        return cp

    def col_sum_3(n, g, cp):
        cp.wait_recv()
        sx, _, _, ring = spot[n]
        _, quart = place(g % 2, sx)
        f, r2 = B[n + "_h"], B[n + "_r2"]
        out = f[g, 1 - quart] + r2[g, 1 - quart].astype(F32)
        B[n + "_s3"][g] = out.astype(B[n + "_s3"].dtype)
        to = dev(x=ring(partners(g % 2, sx)[1]))
        cp = send(B[n + "_s3"].at[g], B[n + "_r3"].at[g], n + "_3", (g,), to)
        B[n + "_q"][g] = f[g, quart] + r2[g, quart].astype(F32)
        return cp

    def col_sum_4(n, g, cp):
        cp.wait_recv()
        sl = spot[n][1]
        f, r3 = B[n + "_q"], B[n + "_r3"]
        out = f[g, 1 - sl] + r3[g, 1 - sl].astype(F32)
        B[n + "_s4"][g] = out.astype(B[n + "_s4"].dtype)
        return send(
            B[n + "_s4"].at[g], B[n + "_r4"].at[g], n + "_4", (g,), dev(l=1 - l)
        )

    def col_sum_end(n, g, cp):
        cp.wait_recv()
        sl = spot[n][1]
        f, r3 = B[n + "_q"], B[n + "_r3"]
        return f[g, sl] + r3[g, sl].astype(F32) + B[n + "_r4"][g].astype(F32)

    def flip(src, dst, sem, g, to):
        cp = pltpu.make_async_remote_copy(
            src_ref=src,
            dst_ref=dst,
            send_sem=S[sem].at[0, g],
            recv_sem=S[sem].at[1, g],
            device_id=to,
        )

        @pl.when(jnp.logical_not(fixed))
        def _():
            cp.start()

        @pl.when(fixed)
        def _():
            dst[...] = src[...]

        pending_flips.append(cp)
        return cp

    def flip_wait(cp):
        @pl.when(jnp.logical_not(fixed))
        def _():
            cp.wait_recv()

    def col_piece(n, g, dx, dl):
        half, quart = place(g % 2, (v + dx) % 4)
        low = ul if dl == 0 else 1 - ul
        return B[n].at[g, 2 * half + quart, low, uk]

    def col_across(n, g, i, piece):
        return send(piece, piece, n + "_g3", (g, i), dev(k=1 - k))

    def col_spread(n, g, dl):
        piece = col_piece(n, g, 0, dl)
        out = {
            (dx, dl): send(piece, piece, n + "_g2", (g, 3 * dl + dx - 1), dev(x=(x + dx) % 4))
            for dx in (1, 3, 2)
        }
        return out, [col_across(n, g, 4 * dl, piece)]

    def col_gather_1(n, g, cp):
        flip_wait(cp)
        piece = col_piece(n, g, 0, 0)
        beside = send(piece, piece, n + "_g1", (g,), dev(l=1 - l))
        return beside, *col_spread(n, g, 0)

    def col_gather_2(n, g, cps):
        beside, out, over = cps
        beside.wait_recv()
        more, too = col_spread(n, g, 1)
        return {**out, **more}, over + too

    def col_gather_3(n, g, cps, dl):
        out, over = cps
        for dx in (1, 3, 2):
            out[dx, dl].wait_recv()
            over.append(col_across(n, g, 4 * dl + dx, col_piece(n, g, dx, dl)))

    def col_gather_end(cps):
        for one in cps[1]:
            one.wait_recv()

    groups = range(GROUPS)
    of_chunk = [(2 * p, 2 * p + 1) for p in range(CHUNKS)]

    cp = {}
    for p in range(CHUNKS):
        for j, (dx, dl) in enumerate(shifts):
            arrive[p][j].wait_recv()
            block = B["sg"].at[p, (x - dx + 4) % 4, (l - dl + 2) % 2, k]
            across[p].append(send(block, block, "ac", (p, j), dev(k=1 - k)))
        for one in across[p]:
            one.wait_recv()
        rows = B["sg"][p].reshape(-1, 2 * LANES)
        split_rows("fp", p, dot(B["co"][...], rows, 0, 0), 64)
        for g in of_chunk[p]:
            cp[g] = bulk_sum_1("fp", g)
    for g in groups:
        cp[g] = bulk_sum_2("fp", g, cp[g])
    for g in groups:
        cp[g] = bulk_sum_3("fp", g, cp[g])
    near, far = {}, {}
    for g in groups:
        half, quart = place(g % 2, y)
        at = (g, 2 * half + quart, hl, hk)
        B["pc"][at] = bulk_sum_end("fp", g, cp[g]).astype(BF)
        far[g] = flip(B["pc"].at[at], B["pr"].at[at], "pr_t", g, flip_to)
    for g in groups:
        near[g] = bulk_gather_1("pc", g)

    for g in groups:
        bulk_gather_3("pc", g, near[g], (0,))
    for g in groups:
        far[g] = col_gather_1("pr", g, far[g])
    for g in groups:
        bulk_gather_2("pc", g, near[g])
    for g in groups:
        far[g] = col_gather_2("pr", g, far[g])
    for g in groups:
        col_gather_3("pr", g, far[g], 0)
    for g in groups:
        bulk_gather_3("pc", g, near[g], (1, 3, 2))
    for g in groups:
        col_gather_3("pr", g, far[g], 1)

    row, col = {}, {}
    for p in range(CHUNKS):
        for g in of_chunk[p]:
            bulk_gather_end(near[g])
        split_rows("fr", p, dot(B["mx"][...], joined("pc", p), 1, 0), 64)
        for g in of_chunk[p]:
            row[g] = col_sum_1("fr", g)
    for p in range(CHUNKS):
        for g in of_chunk[p]:
            col_gather_end(far[g])
        split_rows("fc", p, dot(B["mx"][...], joined("pr", p), 0, 0), 64)
        for g in of_chunk[p]:
            col[g] = bulk_sum_1("fc", g)
        for g in of_chunk[p]:
            row[g] = col_sum_2("fr", g, row[g])
    for g in groups:
        row[g] = col_sum_3("fr", g, row[g])
    for g in groups:
        col[g] = bulk_sum_2("fc", g, col[g])
    for g in groups:
        row[g] = col_sum_4("fr", g, row[g])
    for g in groups:
        B["fr_t"][g] = col_sum_end("fr", g, row[g]).astype(BF)
        row[g] = flip(B["fr_t"].at[g], B["fr_u"].at[g], "fr_t", g, flip_back)
    for g in groups:
        col[g] = bulk_sum_3("fc", g, col[g])
    for g in groups:
        total = bulk_sum_end("fc", g, col[g])
        flip_wait(row[g])
        total = total + B["fr_u"][g].astype(F32)
        half, quart = place(g % 2, y)
        rotated = (0.5 * total).astype(BF)
        B["ro"][g, 2 * half + quart, hl, hk] = rotated
        near[g] = bulk_gather_1("ro", g)
    for g in groups:
        bulk_gather_3("ro", g, near[g], (0,))
    for g in groups:
        bulk_gather_2("ro", g, near[g])
    for g in groups:
        bulk_gather_3("ro", g, near[g], (1, 3, 2))

    for p in range(CHUNKS):
        for g in of_chunk[p]:
            bulk_gather_end(near[g])
        value = dot(B["co"][...], joined("ro", p), 1, 0)
        for g in of_chunk[p]:
            i = g % 2
            part = value[:, i * LANES : (i + 1) * LANES].reshape(4, 2, 2, 96, LANES)
            for v in range(4):
                B["fu"][g, SLOTS[i][v]] = part[v]
            row[g] = col_sum_1("fu", g)
    for g in groups:
        row[g] = col_sum_2("fu", g, row[g])
    for g in groups:
        row[g] = col_sum_3("fu", g, row[g])
    for g in groups:
        row[g] = col_sum_4("fu", g, row[g])
    for g in groups:
        o_ref[:, g * LANES : (g + 1) * LANES] = col_sum_end("fu", g, row[g])
    for one in pending:
        one.wait_send()

    @pl.when(jnp.logical_not(fixed))
    def _():
        for one in pending_flips:
            one.wait_send()


def scratch():
    V = pltpu.VMEM

    def bulk(n, z):
        return {
            n: V((GROUPS, 4, 2, 2, 64, LANES), F32),
            n + "_s1": V((GROUPS, 2, 2, 2, 64, LANES), BF),
            n + "_r1": V((GROUPS, 2, 2, 2, 64, LANES), BF),
            n + "_s2": V((GROUPS, 2, 2, 64, LANES), BF),
            n + "_r2": V((GROUPS, 2, 2, 64, LANES), BF),
            n + "_s3": V((GROUPS, 2, 2, 64, LANES), z),
            n + "_r3": V((GROUPS, 3, 64, LANES), z),
            n + "_own": V((GROUPS, 64, LANES), F32),
        }

    def col(n, rows, t, last):
        return {
            n: V((GROUPS, 4, 2, 2, rows, LANES), F32),
            n + "_r1": V((GROUPS, 4, 2, rows, LANES), F32),
            n + "_h": V((GROUPS, 2, 2, rows, LANES), F32),
            n + "_s2": V((GROUPS, 2, 2, rows, LANES), t),
            n + "_r2": V((GROUPS, 2, 2, rows, LANES), t),
            n + "_q": V((GROUPS, 2, rows, LANES), F32),
            n + "_s3": V((GROUPS, 2, rows, LANES), t),
            n + "_r3": V((GROUPS, 2, rows, LANES), t),
            n + "_s4": V((GROUPS, rows, LANES), last),
            n + "_r4": V((GROUPS, rows, LANES), last),
        }

    whole = (GROUPS, 4, 2, 2, 64, LANES)
    bufs = {
        "sm": V((1024, 1024), BF),
        "sn": V((1024, 1024), BF),
        "mx": V((1024, 1024), BF),
        "co": V((1536, 1024), BF),
        "sg": V((CHUNKS, 4, 2, 2, 96, 2 * LANES), BF),
        "pc": V(whole, BF),
        "pr": V(whole, BF),
        "ro": V(whole, BF),
        "fr_t": V((GROUPS, 64, LANES), BF),
        "fr_u": V((GROUPS, 64, LANES), BF),
        **bulk("fp", BF),
        **bulk("fc", BF),
        **col("fr", 64, BF, F32),
        **col("fu", 96, BF, BF),
    }
    D = pltpu.SemaphoreType.DMA
    sems = {"load": D((3,)), "a": D((2, CHUNKS, 7)), "ac": D((2, CHUNKS, 8))}
    for n in ("fp", "fc"):
        sems.update({n + "_1": D((2, GROUPS)), n + "_2": D((2, GROUPS))})
        sems[n + "_3"] = D((2, GROUPS, 3))
    for n in ("pc", "ro"):
        sems.update({n + "_g2": D((2, GROUPS, 4)), n + "_g3": D((2, GROUPS, 8))})
        sems[n + "_g1"] = D((2, GROUPS, 3))
    for i in range(1, 5):
        for n in ("fr_", "fu_"):
            sems[n + str(i)] = D((2, GROUPS))
    for n in ("pr_g1", "pr_t", "fr_t"):
        sems[n] = D((2, GROUPS))
    sems.update({"pr_g2": D((2, GROUPS, 6)), "pr_g3": D((2, GROUPS, 8))})
    return bufs, sems


def shards(sigma_m, sigma_n, coeffs, s_half):
    bufs, sems = scratch()
    names, sem_names = list(bufs), list(sems)

    def body(*refs):
        rest = refs[5:]
        return kernel(
            *refs[:5],
            dict(zip(names, rest[: len(names)])),
            dict(zip(sem_names, rest[len(names) :])),
        )

    hbm, vmem = pl.BlockSpec(memory_space=pl.ANY), pl.BlockSpec(memory_space=pltpu.VMEM)
    return pl.pallas_call(
        body,
        out_shape=jax.ShapeDtypeStruct(s_half.shape, F32),
        in_specs=[hbm, hbm, hbm, vmem],
        out_specs=vmem,
        scratch_shapes=[*bufs.values(), *sems.values()],
        compiler_params=pltpu.CompilerParams(
            collective_id=0, has_side_effects=True, vmem_limit_bytes=60 << 20
        ),
        name="gw_update",
    )(sigma_m, sigma_n, coeffs, s_half)


def solution(mesh):
    in_specs = (P("bulk", "col"),) * 3 + (P(("bulk", "col"), None),)
    return jax.shard_map(
        shards,
        mesh=mesh,
        in_specs=in_specs,
        out_specs=P(("bulk", "col"), None),
        check_vma=False,
    )
```

```python
import jax
import jax.numpy as jnp
from jax import lax
from jax.experimental import pallas as pl
from jax.experimental.pallas import tpu as pltpu
from jax.sharding import PartitionSpec as P

BF, F32 = jnp.bfloat16, jnp.float32
GROUPS, LANES = 4, 128
CHUNKS = 2
SLOTS = ((0, 2, 3, 1), (0, 1, 2, 3))


def place(colour, v):
    if colour == 0:
        return ((v + 1) // 2) % 2, v // 2
    return v // 2, v % 2


def partners(colour, v):
    near, far = v + 1 - 2 * (v % 2), 3 - v
    return (near, far) if colour == 0 else (far, near)


def dot(a, b, da, db):
    return lax.dot_general(a, b, (((da,), (db,)), ((), ())), preferred_element_type=F32)


def kernel(sm_hbm, sn_hbm, co_hbm, s_ref, o_ref, bufs, sems):
    b, c = lax.axis_index("bulk"), lax.axis_index("col")
    y, h = b // 4, b % 4
    x, l, k = c // 4, (c // 2) % 2, c % 2
    hl, hk = h // 2, h % 2

    def dev(y=y, h=h, x=x, l=l, k=k):
        return {"bulk": y * 4 + h, "col": x * 4 + l * 2 + k}

    w = 2 * l + k
    v, u = (y - x + 4) % 4, (h - w + 4) % 4
    ul, uk = u // 2, u % 2

    flip_to = {"bulk": c, "col": ((x - y + 4) % 4) * 4 + (w - h + 4) % 4}
    flip_back = {"bulk": v * 4 + u, "col": b}

    fixed = (b == 0) & (c == 0)
    B, S = bufs, sems
    pending, pending_flips = [], []

    loads = [
        pltpu.make_async_copy(src, dst, S["load"].at[i])
        for i, (src, dst) in enumerate(
            ((sm_hbm, B["sm"]), (sn_hbm, B["sn"]), (co_hbm, B["co"]))
        )
    ]
    for ld in loads:
        ld.start()

    bar = pltpu.get_barrier_semaphore()
    shifts = [(dx, dl) for dx in range(4) for dl in range(2) if dx or dl]
    peers = [dev(x=(x + dx) % 4, l=(l + dl) % 2) for dx, dl in shifts]
    greeted = peers + [dev(k=1 - k), dev(y=y + 1 - 2 * (y % 2)), dev(y=3 - y)]
    greeted += [dev(h=(h + j) % 4) for j in (1, 2, 3)]
    greeted += [flip_to, flip_back]
    for to in greeted:
        pl.semaphore_signal(bar, inc=1, device_id=to)

    for p in range(CHUNKS):
        B["sg"][p, x, l, k] = s_ref[:, p * 256 : (p + 1) * 256]

    pl.semaphore_wait(bar, len(greeted))

    def send(src, dst, sem, at, to):
        cp = pltpu.make_async_remote_copy(
            src_ref=src,
            dst_ref=dst,
            send_sem=S[sem].at[(0, *at)],
            recv_sem=S[sem].at[(1, *at)],
            device_id=to,
        )
        cp.start()
        pending.append(cp)
        return cp

    own_s = [B["sg"].at[p, x, l, k] for p in range(CHUNKS)]
    arrive = [
        [send(own_s[p], own_s[p], "a", (p, j), to) for j, to in enumerate(peers)]
        for p in range(CHUNKS)
    ]
    across = [
        [send(own_s[p], own_s[p], "ac", (p, 7), dev(k=1 - k))] for p in range(CHUNKS)
    ]

    loads[0].wait()
    loads[1].wait()

    def mix(i, _):
        r = pl.ds(pl.multiple_of(i * 64, 64), 64)
        total = B["sm"][r, :].astype(F32) + B["sn"][r, :].astype(F32)
        B["mx"][r, :] = (0.5 * total).astype(BF)
        return 0

    lax.fori_loop(0, 16, mix, 0)
    loads[2].wait()

    def multiply(name, p, left, da, right, rows):
        for q in range(4):
            r = slice(4 * rows * q, 4 * rows * (q + 1))
            part = B[left][:, r] if da == 0 else B[left][r, :]
            value = dot(part, right, da, 0)
            for i in range(2):
                slot = SLOTS[i][q] if name == "fu" else q
                tile = value[:, i * LANES : (i + 1) * LANES]
                B[name][2 * p + i, slot] = tile.reshape(2, 2, rows, LANES)

    def joined(name, p):
        return jnp.concatenate(
            [B[name][2 * p + i].reshape(-1, LANES) for i in range(2)], axis=1
        )

    def bulk_sum_1(n, g):
        half, _ = place(g % 2, y)
        B[n + "_s1"][g] = B[n][g, pl.ds(2 * (1 - half), 2)].astype(BF)
        to = dev(y=partners(g % 2, y)[0])
        return send(B[n + "_s1"].at[g], B[n + "_r1"].at[g], n + "_1", (g,), to)

    def bulk_sum_2(n, g, cp):
        cp.wait_recv()
        half, quart = place(g % 2, y)
        f, r1 = B[n], B[n + "_r1"]
        other = f[g, 2 * half + 1 - quart] + r1[g, 1 - quart].astype(F32)
        B[n + "_s2"][g] = other.astype(BF)
        to = dev(y=partners(g % 2, y)[1])
        cp = send(B[n + "_s2"].at[g], B[n + "_r2"].at[g], n + "_2", (g,), to)
        f[g, 2 * half + quart] = f[g, 2 * half + quart] + r1[g, quart].astype(F32)
        return cp

    def bulk_sum_3(n, g, cp):
        cp.wait_recv()
        half, quart = place(g % 2, y)
        total = B[n][g, 2 * half + quart] + B[n + "_r2"][g].astype(F32)
        B[n + "_s3"][g] = total.astype(B[n + "_s3"].dtype)
        cps = []
        for j in (1, 2, 3):
            to = (h + j) % 4
            cps.append(
                send(
                    B[n + "_s3"].at[g, to // 2, to % 2],
                    B[n + "_r3"].at[g, j - 1],
                    n + "_3",
                    (g, j - 1),
                    dev(h=to),
                )
            )
        own = B[n][g, 2 * half + quart, hl, hk]
        B[n + "_own"][g] = own + B[n + "_r2"][g, hl, hk].astype(F32)
        return cps

    def bulk_sum_end(n, g, cps):
        for cp in cps:
            cp.wait_recv()
        r3 = B[n + "_r3"]
        total = B[n + "_own"][g] + r3[g, 0].astype(F32)
        return total + (r3[g, 1].astype(F32) + r3[g, 2].astype(F32))

    def bulk_gather_1(n, g):
        half, quart = place(g % 2, y)
        piece = B[n].at[g, 2 * half + quart, hl, hk]
        first, second = partners(g % 2, y)
        z = {
            j: send(piece, piece, n + "_g1", (g, j - 1), dev(h=(h + j) % 4))
            for j in (1, 3, 2)
        }
        y2 = {0: send(piece, piece, n + "_g2", (g, 0), dev(y=second))}
        y1 = {0: send(piece, piece, n + "_g3", (g, 0), dev(y=first))}
        return z, y2, y1

    def bulk_gather_2(n, g, cps):
        z, y2, y1 = cps
        half, quart = place(g % 2, y)
        first, second = partners(g % 2, y)
        for j in (1, 3, 2):
            z[j].wait_recv()
            at = (h - j + 4) % 4
            piece = B[n].at[g, 2 * half + quart, at // 2, at % 2]
            y2[j] = send(piece, piece, n + "_g2", (g, j), dev(y=second))
            y1[j] = send(piece, piece, n + "_g3", (g, j), dev(y=first))

    def bulk_gather_3(n, g, cps, which):
        _, y2, y1 = cps
        half, quart = place(g % 2, y)
        first, _ = partners(g % 2, y)
        for j in which:
            y2[j].wait_recv()
            at = (h - j + 4) % 4
            piece = B[n].at[g, 2 * half + 1 - quart, at // 2, at % 2]
            y1[4 + j] = send(piece, piece, n + "_g3", (g, 4 + j), dev(y=first))

    def bulk_gather_end(cps):
        for j in range(8):
            cps[2][j].wait_recv()

    def row_sum_2(g, cp):
        cp.wait_recv()
        total = B["fr"][g, :, :, uk] + B["fr_r1"][g]
        B["fr_h"][g] = total
        B["fr_s2"][g] = total.astype(BF)
        cps = []
        for i, (dx, dl) in enumerate(shifts):
            half, quart = place(g % 2, (v - dx + 4) % 4)
            low = 1 - ul if dl else ul
            piece = B["fr_s2"].at[g, 2 * half + quart, low]
            cps.append(send(piece, B["fr_r2"].at[g, i], "fr_2", (g, i), peers[i]))
        return cps

    def row_sum_end(g, cps):
        half, quart = place(g % 2, v)
        total = B["fr_h"][g, 2 * half + quart, ul]
        for i, one in enumerate(cps):
            one.wait_recv()
            total = total + B["fr_r2"][g, i].astype(F32)
        return total

    plain = (x, l, k, lambda at: at)
    turned = (v, ul, uk, lambda at: (y - at + 4) % 4)
    spot = {"fu": plain, "fr": turned}

    def col_sum_1(n, g):
        _, _, sk, _ = spot[n]
        return send(
            B[n].at[g, :, :, 1 - sk], B[n + "_r1"].at[g], n + "_1", (g,), dev(k=1 - k)
        )

    def col_sum_2(n, g, cp):
        cp.wait_recv()
        sx, _, sk, ring = spot[n]
        half, _ = place(g % 2, sx)
        f, r1, away = B[n], B[n + "_r1"], pl.ds(2 * (1 - half), 2)
        out = f[g, away, :, sk] + r1[g, away]
        B[n + "_s2"][g] = out.astype(B[n + "_s2"].dtype)
        to = dev(x=ring(partners(g % 2, sx)[0]))
        cp = send(B[n + "_s2"].at[g], B[n + "_r2"].at[g], n + "_2", (g,), to)
        here = pl.ds(2 * half, 2)
        B[n + "_h"][g] = f[g, here, :, sk] + r1[g, here]
        return cp

    def col_sum_3(n, g, cp):
        cp.wait_recv()
        sx, _, _, ring = spot[n]
        _, quart = place(g % 2, sx)
        f, r2 = B[n + "_h"], B[n + "_r2"]
        out = f[g, 1 - quart] + r2[g, 1 - quart].astype(F32)
        B[n + "_s3"][g] = out.astype(B[n + "_s3"].dtype)
        to = dev(x=ring(partners(g % 2, sx)[1]))
        cp = send(B[n + "_s3"].at[g], B[n + "_r3"].at[g], n + "_3", (g,), to)
        B[n + "_q"][g] = f[g, quart] + r2[g, quart].astype(F32)
        return cp

    def col_sum_4(n, g, cp):
        cp.wait_recv()
        sl = spot[n][1]
        f, r3 = B[n + "_q"], B[n + "_r3"]
        out = f[g, 1 - sl] + r3[g, 1 - sl].astype(F32)
        B[n + "_s4"][g] = out.astype(B[n + "_s4"].dtype)
        return send(
            B[n + "_s4"].at[g], B[n + "_r4"].at[g], n + "_4", (g,), dev(l=1 - l)
        )

    def col_sum_end(n, g, cp):
        cp.wait_recv()
        sl = spot[n][1]
        f, r3 = B[n + "_q"], B[n + "_r3"]
        return f[g, sl] + r3[g, sl].astype(F32) + B[n + "_r4"][g].astype(F32)

    def flip(src, dst, sem, g, to):
        cp = pltpu.make_async_remote_copy(
            src_ref=src,
            dst_ref=dst,
            send_sem=S[sem].at[0, g],
            recv_sem=S[sem].at[1, g],
            device_id=to,
        )

        @pl.when(jnp.logical_not(fixed))
        def _():
            cp.start()

        @pl.when(fixed)
        def _():
            dst[...] = src[...]

        pending_flips.append(cp)
        return cp

    def flip_wait(cp):
        @pl.when(jnp.logical_not(fixed))
        def _():
            cp.wait_recv()

    def col_piece(n, g, dx, dl):
        half, quart = place(g % 2, (v + dx) % 4)
        low = ul if dl == 0 else 1 - ul
        return B[n].at[g, 2 * half + quart, low, uk]

    def col_across(n, g, i, piece):
        return send(piece, piece, n + "_g3", (g, i), dev(k=1 - k))

    def col_spread(n, g, dl):
        piece = col_piece(n, g, 0, dl)
        out = {
            (dx, dl): send(piece, piece, n + "_g2", (g, 3 * dl + dx - 1), dev(x=(x + dx) % 4))
            for dx in (1, 3, 2)
        }
        return out, [col_across(n, g, 4 * dl, piece)]

    def col_gather_1(n, g, cp):
        flip_wait(cp)
        piece = col_piece(n, g, 0, 0)
        beside = send(piece, piece, n + "_g1", (g,), dev(l=1 - l))
        return beside, *col_spread(n, g, 0)

    def col_gather_2(n, g, cps):
        beside, out, over = cps
        beside.wait_recv()
        more, too = col_spread(n, g, 1)
        return {**out, **more}, over + too

    def col_gather_3(n, g, cps, dl):
        out, over = cps
        for dx in (1, 3, 2):
            out[dx, dl].wait_recv()
            over.append(col_across(n, g, 4 * dl + dx, col_piece(n, g, dx, dl)))

    def col_gather_end(cps):
        for one in cps[1]:
            one.wait_recv()

    groups = range(GROUPS)
    of_chunk = [(2 * p, 2 * p + 1) for p in range(CHUNKS)]

    cp = {}
    for p in range(CHUNKS):
        for j, (dx, dl) in enumerate(shifts):
            arrive[p][j].wait_recv()
            block = B["sg"].at[p, (x - dx + 4) % 4, (l - dl + 2) % 2, k]
            across[p].append(send(block, block, "ac", (p, j), dev(k=1 - k)))
        for one in across[p]:
            one.wait_recv()
        rows = B["sg"][p].reshape(-1, 2 * LANES)
        multiply("fp", p, "co", 0, rows, 64)
        for g in of_chunk[p]:
            cp[g] = bulk_sum_1("fp", g)
    for g in groups:
        cp[g] = bulk_sum_2("fp", g, cp[g])
    for g in groups:
        cp[g] = bulk_sum_3("fp", g, cp[g])
    near, far = {}, {}
    for g in groups:
        half, quart = place(g % 2, y)
        at = (g, 2 * half + quart, hl, hk)
        B["pc"][at] = bulk_sum_end("fp", g, cp[g]).astype(BF)
        far[g] = flip(B["pc"].at[at], B["pr"].at[at], "pr_t", g, flip_to)
    for g in groups:
        near[g] = bulk_gather_1("pc", g)

    for g in groups:
        bulk_gather_3("pc", g, near[g], (0,))
    for g in groups:
        far[g] = col_gather_1("pr", g, far[g])
    for g in groups:
        bulk_gather_2("pc", g, near[g])
    for g in groups:
        far[g] = col_gather_2("pr", g, far[g])
    for g in groups:
        col_gather_3("pr", g, far[g], 0)
    for g in groups:
        bulk_gather_3("pc", g, near[g], (1, 3, 2))
    for g in groups:
        col_gather_3("pr", g, far[g], 1)

    row, col = {}, {}
    for p in range(CHUNKS):
        for g in of_chunk[p]:
            bulk_gather_end(near[g])
        multiply("fr", p, "mx", 1, joined("pc", p), 64)
        for g in of_chunk[p]:
            row[g] = col_sum_1("fr", g)
    for p in range(CHUNKS):
        for g in of_chunk[p]:
            col_gather_end(far[g])
        multiply("fc", p, "mx", 0, joined("pr", p), 64)
        for g in of_chunk[p]:
            col[g] = bulk_sum_1("fc", g)
        for g in of_chunk[p]:
            row[g] = row_sum_2(g, row[g])
    for g in groups:
        col[g] = bulk_sum_2("fc", g, col[g])
    for g in groups:
        B["fr_t"][g] = row_sum_end(g, row[g]).astype(BF)
        row[g] = flip(B["fr_t"].at[g], B["fr_u"].at[g], "fr_t", g, flip_back)
    for g in groups:
        col[g] = bulk_sum_3("fc", g, col[g])
    for g in groups:
        total = bulk_sum_end("fc", g, col[g])
        flip_wait(row[g])
        total = total + B["fr_u"][g].astype(F32)
        half, quart = place(g % 2, y)
        rotated = (0.5 * total).astype(BF)
        B["ro"][g, 2 * half + quart, hl, hk] = rotated
        near[g] = bulk_gather_1("ro", g)
    for g in groups:
        bulk_gather_3("ro", g, near[g], (0,))
    for g in groups:
        bulk_gather_2("ro", g, near[g])
    for g in groups:
        bulk_gather_3("ro", g, near[g], (1, 3, 2))

    for p in range(CHUNKS):
        for g in of_chunk[p]:
            bulk_gather_end(near[g])
        multiply("fu", p, "co", 1, joined("ro", p), 96)
        for g in of_chunk[p]:
            row[g] = col_sum_1("fu", g)
    for g in groups:
        row[g] = col_sum_2("fu", g, row[g])
    for g in groups:
        row[g] = col_sum_3("fu", g, row[g])
    for g in groups:
        row[g] = col_sum_4("fu", g, row[g])
    for g in groups:
        o_ref[:, g * LANES : (g + 1) * LANES] = col_sum_end("fu", g, row[g])
    for one in pending:
        one.wait_send()

    @pl.when(jnp.logical_not(fixed))
    def _():
        for one in pending_flips:
            one.wait_send()


def scratch():
    V = pltpu.VMEM

    def bulk(n, z):
        return {
            n: V((GROUPS, 4, 2, 2, 64, LANES), F32),
            n + "_s1": V((GROUPS, 2, 2, 2, 64, LANES), BF),
            n + "_r1": V((GROUPS, 2, 2, 2, 64, LANES), BF),
            n + "_s2": V((GROUPS, 2, 2, 64, LANES), BF),
            n + "_r2": V((GROUPS, 2, 2, 64, LANES), BF),
            n + "_s3": V((GROUPS, 2, 2, 64, LANES), z),
            n + "_r3": V((GROUPS, 3, 64, LANES), z),
            n + "_own": V((GROUPS, 64, LANES), F32),
        }

    def col(n, rows, t, last):
        return {
            n: V((GROUPS, 4, 2, 2, rows, LANES), F32),
            n + "_r1": V((GROUPS, 4, 2, rows, LANES), F32),
            n + "_h": V((GROUPS, 2, 2, rows, LANES), F32),
            n + "_s2": V((GROUPS, 2, 2, rows, LANES), t),
            n + "_r2": V((GROUPS, 2, 2, rows, LANES), t),
            n + "_q": V((GROUPS, 2, rows, LANES), F32),
            n + "_s3": V((GROUPS, 2, rows, LANES), t),
            n + "_r3": V((GROUPS, 2, rows, LANES), t),
            n + "_s4": V((GROUPS, rows, LANES), last),
            n + "_r4": V((GROUPS, rows, LANES), last),
        }

    whole = (GROUPS, 4, 2, 2, 64, LANES)
    bufs = {
        "sm": V((1024, 1024), BF),
        "sn": V((1024, 1024), BF),
        "mx": V((1024, 1024), BF),
        "co": V((1536, 1024), BF),
        "sg": V((CHUNKS, 4, 2, 2, 96, 2 * LANES), BF),
        "pc": V(whole, BF),
        "pr": V(whole, BF),
        "ro": V(whole, BF),
        "fr_t": V((GROUPS, 64, LANES), BF),
        "fr_u": V((GROUPS, 64, LANES), BF),
        **bulk("fp", BF),
        **bulk("fc", BF),
        "fr": V(whole, F32),
        "fr_r1": V((GROUPS, 4, 2, 64, LANES), F32),
        "fr_h": V((GROUPS, 4, 2, 64, LANES), F32),
        "fr_s2": V((GROUPS, 4, 2, 64, LANES), BF),
        "fr_r2": V((GROUPS, 7, 64, LANES), BF),
        **col("fu", 96, BF, BF),
    }
    D = pltpu.SemaphoreType.DMA
    sems = {"load": D((3,)), "a": D((2, CHUNKS, 7)), "ac": D((2, CHUNKS, 8))}
    for n in ("fp", "fc"):
        sems.update({n + "_1": D((2, GROUPS)), n + "_2": D((2, GROUPS))})
        sems[n + "_3"] = D((2, GROUPS, 3))
    for n in ("pc", "ro"):
        sems.update({n + "_g2": D((2, GROUPS, 4)), n + "_g3": D((2, GROUPS, 8))})
        sems[n + "_g1"] = D((2, GROUPS, 3))
    for i in range(1, 5):
        sems["fu_" + str(i)] = D((2, GROUPS))
    sems["fr_2"] = D((2, GROUPS, 7))
    for n in ("pr_g1", "pr_t", "fr_t", "fr_1"):
        sems[n] = D((2, GROUPS))
    sems.update({"pr_g2": D((2, GROUPS, 6)), "pr_g3": D((2, GROUPS, 8))})
    return bufs, sems


def shards(sigma_m, sigma_n, coeffs, s_half):
    bufs, sems = scratch()
    names, sem_names = list(bufs), list(sems)

    def body(*refs):
        rest = refs[5:]
        return kernel(
            *refs[:5],
            dict(zip(names, rest[: len(names)])),
            dict(zip(sem_names, rest[len(names) :])),
        )

    hbm, vmem = pl.BlockSpec(memory_space=pl.ANY), pl.BlockSpec(memory_space=pltpu.VMEM)
    return pl.pallas_call(
        body,
        out_shape=jax.ShapeDtypeStruct(s_half.shape, F32),
        in_specs=[hbm, hbm, hbm, vmem],
        out_specs=vmem,
        scratch_shapes=[*bufs.values(), *sems.values()],
        compiler_params=pltpu.CompilerParams(
            collective_id=0, has_side_effects=True, vmem_limit_bytes=60 << 20
        ),
        name="gw_update",
    )(sigma_m, sigma_n, coeffs, s_half)


def solution(mesh):
    in_specs = (P("bulk", "col"),) * 3 + (P(("bulk", "col"), None),)
    return jax.shard_map(
        shards,
        mesh=mesh,
        in_specs=in_specs,
        out_specs=P(("bulk", "col"), None),
        check_vma=False,
    )
```

```python
import jax
import jax.numpy as jnp
from jax import lax
from jax.experimental import pallas as pl
from jax.experimental.pallas import tpu as pltpu
from jax.sharding import PartitionSpec as P

BF, F32 = jnp.bfloat16, jnp.float32
GROUPS, LANES = 4, 128
CHUNKS = 2
SLOTS = ((0, 2, 3, 1), (0, 1, 2, 3))


def place(colour, v):
    if colour == 0:
        return ((v + 1) // 2) % 2, v // 2
    return v // 2, v % 2


def partners(colour, v):
    near, far = v + 1 - 2 * (v % 2), 3 - v
    return (near, far) if colour == 0 else (far, near)


def dot(a, b, da, db):
    return lax.dot_general(a, b, (((da,), (db,)), ((), ())), preferred_element_type=F32)


def kernel(sm_hbm, sn_hbm, co_hbm, s_ref, o_ref, bufs, sems):
    b, c = lax.axis_index("bulk"), lax.axis_index("col")
    y, h = b // 4, b % 4
    x, l, k = c // 4, (c // 2) % 2, c % 2
    hl, hk = h // 2, h % 2

    def dev(y=y, h=h, x=x, l=l, k=k):
        return {"bulk": y * 4 + h, "col": x * 4 + l * 2 + k}

    w = 2 * l + k
    v, u = (y - x + 4) % 4, (h - w + 4) % 4
    ul, uk = u // 2, u % 2

    flip_to = {"bulk": c, "col": ((x - y + 4) % 4) * 4 + (w - h + 4) % 4}
    flip_back = {"bulk": v * 4 + u, "col": b}

    fixed = (b == 0) & (c == 0)
    B, S = bufs, sems
    pending, pending_flips = [], []

    loads = [
        pltpu.make_async_copy(src, dst, S["load"].at[i])
        for i, (src, dst) in enumerate(
            ((sm_hbm, B["sm"]), (sn_hbm, B["sn"]), (co_hbm, B["co"]))
        )
    ]
    for ld in loads:
        ld.start()

    bar = pltpu.get_barrier_semaphore()
    shifts = [(dx, dl) for dx in range(4) for dl in range(2) if dx or dl]
    peers = [dev(x=(x + dx) % 4, l=(l + dl) % 2) for dx, dl in shifts]
    greeted = peers + [dev(k=1 - k), dev(y=y + 1 - 2 * (y % 2)), dev(y=3 - y)]
    greeted += [dev(h=(h + j) % 4) for j in (1, 2, 3)]
    greeted += [flip_to, flip_back]
    for to in greeted:
        pl.semaphore_signal(bar, inc=1, device_id=to)

    for p in range(CHUNKS):
        B["sg"][p, x, l, k] = s_ref[:, p * 256 : (p + 1) * 256]

    pl.semaphore_wait(bar, len(greeted))

    def send(src, dst, sem, at, to):
        cp = pltpu.make_async_remote_copy(
            src_ref=src,
            dst_ref=dst,
            send_sem=S[sem].at[(0, *at)],
            recv_sem=S[sem].at[(1, *at)],
            device_id=to,
        )
        cp.start()
        pending.append(cp)
        return cp

    own_s = [B["sg"].at[p, x, l, k] for p in range(CHUNKS)]
    arrive = [
        [send(own_s[p], own_s[p], "a", (p, j), to) for j, to in enumerate(peers)]
        for p in range(CHUNKS)
    ]
    across = [
        [send(own_s[p], own_s[p], "ac", (p, 7), dev(k=1 - k))] for p in range(CHUNKS)
    ]

    loads[0].wait()
    loads[1].wait()

    def mix(i, _):
        r = pl.ds(pl.multiple_of(i * 64, 64), 64)
        total = B["sm"][r, :].astype(F32) + B["sn"][r, :].astype(F32)
        B["mx"][r, :] = (0.5 * total).astype(BF)
        return 0

    lax.fori_loop(0, 16, mix, 0)
    loads[2].wait()

    def multiply(name, p, left, da, right, rows):
        for q in range(4):
            r = slice(4 * rows * q, 4 * rows * (q + 1))
            part = B[left][:, r] if da == 0 else B[left][r, :]
            value = dot(part, right, da, 0)
            for i in range(2):
                slot = SLOTS[i][q] if name == "fu" else q
                tile = value[:, i * LANES : (i + 1) * LANES]
                B[name][2 * p + i, slot] = tile.reshape(2, 2, rows, LANES)

    def joined(name, p):
        return jnp.concatenate(
            [B[name][2 * p + i].reshape(-1, LANES) for i in range(2)], axis=1
        )

    def bulk_sum_1(n, g):
        half, _ = place(g % 2, y)
        B[n + "_s1"][g] = B[n][g, pl.ds(2 * (1 - half), 2)].astype(BF)
        to = dev(y=partners(g % 2, y)[0])
        return send(B[n + "_s1"].at[g], B[n + "_r1"].at[g], n + "_1", (g,), to)

    def bulk_sum_2(n, g, cp):
        cp.wait_recv()
        half, quart = place(g % 2, y)
        f, r1 = B[n], B[n + "_r1"]
        other = f[g, 2 * half + 1 - quart] + r1[g, 1 - quart].astype(F32)
        B[n + "_s2"][g] = other.astype(BF)
        to = dev(y=partners(g % 2, y)[1])
        cp = send(B[n + "_s2"].at[g], B[n + "_r2"].at[g], n + "_2", (g,), to)
        f[g, 2 * half + quart] = f[g, 2 * half + quart] + r1[g, quart].astype(F32)
        return cp

    def bulk_sum_3(n, g, cp):
        cp.wait_recv()
        half, quart = place(g % 2, y)
        total = B[n][g, 2 * half + quart] + B[n + "_r2"][g].astype(F32)
        B[n + "_s3"][g] = total.astype(B[n + "_s3"].dtype)
        cps = []
        for j in (1, 2, 3):
            to = (h + j) % 4
            cps.append(
                send(
                    B[n + "_s3"].at[g, to // 2, to % 2],
                    B[n + "_r3"].at[g, j - 1],
                    n + "_3",
                    (g, j - 1),
                    dev(h=to),
                )
            )
        own = B[n][g, 2 * half + quart, hl, hk]
        B[n + "_own"][g] = own + B[n + "_r2"][g, hl, hk].astype(F32)
        return cps

    def bulk_sum_end(n, g, cps):
        for cp in cps:
            cp.wait_recv()
        r3 = B[n + "_r3"]
        total = B[n + "_own"][g] + r3[g, 0].astype(F32)
        return total + (r3[g, 1].astype(F32) + r3[g, 2].astype(F32))

    def bulk_gather_1(n, g):
        half, quart = place(g % 2, y)
        piece = B[n].at[g, 2 * half + quart, hl, hk]
        first, second = partners(g % 2, y)
        z = {
            j: send(piece, piece, n + "_g1", (g, j - 1), dev(h=(h + j) % 4))
            for j in (1, 3, 2)
        }
        y2 = {0: send(piece, piece, n + "_g2", (g, 0), dev(y=second))}
        y1 = {0: send(piece, piece, n + "_g3", (g, 0), dev(y=first))}
        return z, y2, y1

    def bulk_gather_2(n, g, cps):
        z, y2, y1 = cps
        half, quart = place(g % 2, y)
        first, second = partners(g % 2, y)
        for j in (1, 3, 2):
            z[j].wait_recv()
            at = (h - j + 4) % 4
            piece = B[n].at[g, 2 * half + quart, at // 2, at % 2]
            y2[j] = send(piece, piece, n + "_g2", (g, j), dev(y=second))
            y1[j] = send(piece, piece, n + "_g3", (g, j), dev(y=first))

    def bulk_gather_3(n, g, cps, which):
        _, y2, y1 = cps
        half, quart = place(g % 2, y)
        first, _ = partners(g % 2, y)
        for j in which:
            y2[j].wait_recv()
            at = (h - j + 4) % 4
            piece = B[n].at[g, 2 * half + 1 - quart, at // 2, at % 2]
            y1[4 + j] = send(piece, piece, n + "_g3", (g, 4 + j), dev(y=first))

    def bulk_gather_end(cps):
        for j in range(8):
            cps[2][j].wait_recv()

    def col_sum_2(n, g, cp):
        cp.wait_recv()
        sx, sl, sk, sign = spot[n]
        total = B[n][g, :, :, sk] + B[n + "_r1"][g].astype(F32)
        B[n + "_h"][g] = total
        B[n + "_s2"][g] = total.astype(BF)
        cps = []
        for i, (dx, dl) in enumerate(shifts):
            half, quart = place(g % 2, (sx + sign * dx + 4) % 4)
            piece = B[n + "_s2"].at[g, 2 * half + quart, 1 - sl if dl else sl]
            cps.append(send(piece, B[n + "_r2"].at[g, i], n + "_2", (g, i), peers[i]))
        return cps

    def col_sum_end(n, g, cps):
        sx, sl, _, _ = spot[n]
        half, quart = place(g % 2, sx)
        total = B[n + "_h"][g, 2 * half + quart, sl]
        for i, one in enumerate(cps):
            one.wait_recv()
            total = total + B[n + "_r2"][g, i].astype(F32)
        return total

    spot = {"fu": (x, l, k, 1), "fr": (v, ul, uk, -1)}

    def col_sum_1(n, g):
        away = 1 - spot[n][2]
        src = B[n].at[g, :, :, away]
        return send(src, B[n + "_r1"].at[g], n + "_1", (g,), dev(k=1 - k))

    def flip(src, dst, sem, g, to):
        cp = pltpu.make_async_remote_copy(
            src_ref=src,
            dst_ref=dst,
            send_sem=S[sem].at[0, g],
            recv_sem=S[sem].at[1, g],
            device_id=to,
        )

        @pl.when(jnp.logical_not(fixed))
        def _():
            cp.start()

        @pl.when(fixed)
        def _():
            dst[...] = src[...]

        pending_flips.append(cp)
        return cp

    def flip_wait(cp):
        @pl.when(jnp.logical_not(fixed))
        def _():
            cp.wait_recv()

    def col_piece(n, g, dx, dl):
        half, quart = place(g % 2, (v + dx) % 4)
        low = ul if dl == 0 else 1 - ul
        return B[n].at[g, 2 * half + quart, low, uk]

    def col_across(n, g, i, piece):
        return send(piece, piece, n + "_g3", (g, i), dev(k=1 - k))

    def col_spread(n, g, dl):
        piece = col_piece(n, g, 0, dl)
        out = {
            (dx, dl): send(piece, piece, n + "_g2", (g, 3 * dl + dx - 1), dev(x=(x + dx) % 4))
            for dx in (1, 3, 2)
        }
        return out, [col_across(n, g, 4 * dl, piece)]

    def col_gather_1(n, g, cp):
        flip_wait(cp)
        piece = col_piece(n, g, 0, 0)
        beside = send(piece, piece, n + "_g1", (g,), dev(l=1 - l))
        return beside, *col_spread(n, g, 0)

    def col_gather_2(n, g, cps):
        beside, out, over = cps
        beside.wait_recv()
        more, too = col_spread(n, g, 1)
        return {**out, **more}, over + too

    def col_gather_3(n, g, cps, dl):
        out, over = cps
        for dx in (1, 3, 2):
            out[dx, dl].wait_recv()
            over.append(col_across(n, g, 4 * dl + dx, col_piece(n, g, dx, dl)))

    def col_gather_end(cps):
        for one in cps[1]:
            one.wait_recv()

    groups = range(GROUPS)
    of_chunk = [(2 * p, 2 * p + 1) for p in range(CHUNKS)]

    cp = {}
    for p in range(CHUNKS):
        for j, (dx, dl) in enumerate(shifts):
            arrive[p][j].wait_recv()
            block = B["sg"].at[p, (x - dx + 4) % 4, (l - dl + 2) % 2, k]
            across[p].append(send(block, block, "ac", (p, j), dev(k=1 - k)))
        for one in across[p]:
            one.wait_recv()
        rows = B["sg"][p].reshape(-1, 2 * LANES)
        multiply("fp", p, "co", 0, rows, 64)
        for g in of_chunk[p]:
            cp[g] = bulk_sum_1("fp", g)
    for g in groups:
        cp[g] = bulk_sum_2("fp", g, cp[g])
    for g in groups:
        cp[g] = bulk_sum_3("fp", g, cp[g])
    near, far = {}, {}
    for g in groups:
        half, quart = place(g % 2, y)
        at = (g, 2 * half + quart, hl, hk)
        B["pc"][at] = bulk_sum_end("fp", g, cp[g]).astype(BF)
        far[g] = flip(B["pc"].at[at], B["pr"].at[at], "pr_t", g, flip_to)
    for g in groups:
        near[g] = bulk_gather_1("pc", g)

    for g in groups:
        bulk_gather_3("pc", g, near[g], (0,))
    for g in groups:
        far[g] = col_gather_1("pr", g, far[g])
    for g in groups:
        bulk_gather_2("pc", g, near[g])
    for g in groups:
        far[g] = col_gather_2("pr", g, far[g])
    for g in groups:
        col_gather_3("pr", g, far[g], 0)
    for g in groups:
        bulk_gather_3("pc", g, near[g], (1, 3, 2))
    for g in groups:
        col_gather_3("pr", g, far[g], 1)

    row, col = {}, {}
    for p in range(CHUNKS):
        for g in of_chunk[p]:
            bulk_gather_end(near[g])
        multiply("fr", p, "mx", 1, joined("pc", p), 64)
        for g in of_chunk[p]:
            row[g] = col_sum_1("fr", g)
    for g in groups:
        row[g] = col_sum_2("fr", g, row[g])
    for p in range(CHUNKS):
        for g in of_chunk[p]:
            col_gather_end(far[g])
        multiply("fc", p, "mx", 0, joined("pr", p), 64)
        for g in of_chunk[p]:
            col[g] = bulk_sum_1("fc", g)
    for g in groups:
        col[g] = bulk_sum_2("fc", g, col[g])
    for g in groups:
        B["fr_t"][g] = col_sum_end("fr", g, row[g]).astype(BF)
        row[g] = flip(B["fr_t"].at[g], B["fr_u"].at[g], "fr_t", g, flip_back)
    for g in groups:
        col[g] = bulk_sum_3("fc", g, col[g])
    for g in groups:
        total = bulk_sum_end("fc", g, col[g])
        flip_wait(row[g])
        total = total + B["fr_u"][g].astype(F32)
        half, quart = place(g % 2, y)
        rotated = (0.5 * total).astype(BF)
        B["ro"][g, 2 * half + quart, hl, hk] = rotated
        near[g] = bulk_gather_1("ro", g)
    for g in groups:
        bulk_gather_3("ro", g, near[g], (0,))
    for g in groups:
        bulk_gather_2("ro", g, near[g])
    for g in groups:
        bulk_gather_3("ro", g, near[g], (1, 3, 2))

    for p in range(CHUNKS):
        for g in of_chunk[p]:
            bulk_gather_end(near[g])
        multiply("fu", p, "co", 1, joined("ro", p), 96)
        for g in of_chunk[p]:
            row[g] = col_sum_1("fu", g)
    for g in groups:
        row[g] = col_sum_2("fu", g, row[g])
    for g in groups:
        o_ref[:, g * LANES : (g + 1) * LANES] = col_sum_end("fu", g, row[g])
    for one in pending:
        one.wait_send()

    @pl.when(jnp.logical_not(fixed))
    def _():
        for one in pending_flips:
            one.wait_send()


def scratch():
    V = pltpu.VMEM

    def bulk(n, z):
        return {
            n: V((GROUPS, 4, 2, 2, 64, LANES), F32),
            n + "_s1": V((GROUPS, 2, 2, 2, 64, LANES), BF),
            n + "_r1": V((GROUPS, 2, 2, 2, 64, LANES), BF),
            n + "_s2": V((GROUPS, 2, 2, 64, LANES), BF),
            n + "_r2": V((GROUPS, 2, 2, 64, LANES), BF),
            n + "_s3": V((GROUPS, 2, 2, 64, LANES), z),
            n + "_r3": V((GROUPS, 3, 64, LANES), z),
            n + "_own": V((GROUPS, 64, LANES), F32),
        }

    def col(n, rows, t):
        return {
            n: V((GROUPS, 4, 2, 2, rows, LANES), F32),
            n + "_s1": V((GROUPS, 4, 2, rows, LANES), t),
            n + "_r1": V((GROUPS, 4, 2, rows, LANES), t),
            n + "_h": V((GROUPS, 4, 2, rows, LANES), F32),
            n + "_s2": V((GROUPS, 4, 2, rows, LANES), BF),
            n + "_r2": V((GROUPS, 7, rows, LANES), BF),
        }

    whole = (GROUPS, 4, 2, 2, 64, LANES)
    bufs = {
        "sm": V((1024, 1024), BF),
        "sn": V((1024, 1024), BF),
        "mx": V((1024, 1024), BF),
        "co": V((1536, 1024), BF),
        "sg": V((CHUNKS, 4, 2, 2, 96, 2 * LANES), BF),
        "pc": V(whole, BF),
        "pr": V(whole, BF),
        "ro": V(whole, BF),
        "fr_t": V((GROUPS, 64, LANES), BF),
        "fr_u": V((GROUPS, 64, LANES), BF),
        **bulk("fp", BF),
        **bulk("fc", BF),
        **col("fr", 64, F32),
        **col("fu", 96, F32),
    }
    D = pltpu.SemaphoreType.DMA
    sems = {"load": D((3,)), "a": D((2, CHUNKS, 7)), "ac": D((2, CHUNKS, 8))}
    for n in ("fp", "fc"):
        sems.update({n + "_1": D((2, GROUPS)), n + "_2": D((2, GROUPS))})
        sems[n + "_3"] = D((2, GROUPS, 3))
    for n in ("pc", "ro"):
        sems.update({n + "_g2": D((2, GROUPS, 4)), n + "_g3": D((2, GROUPS, 8))})
        sems[n + "_g1"] = D((2, GROUPS, 3))
    sems["fr_2"] = D((2, GROUPS, 7))
    sems["fu_2"] = D((2, GROUPS, 7))
    for n in ("pr_g1", "pr_t", "fr_t", "fr_1", "fu_1"):
        sems[n] = D((2, GROUPS))
    sems.update({"pr_g2": D((2, GROUPS, 6)), "pr_g3": D((2, GROUPS, 8))})
    return bufs, sems


def shards(sigma_m, sigma_n, coeffs, s_half):
    bufs, sems = scratch()
    names, sem_names = list(bufs), list(sems)

    def body(*refs):
        rest = refs[5:]
        return kernel(
            *refs[:5],
            dict(zip(names, rest[: len(names)])),
            dict(zip(sem_names, rest[len(names) :])),
        )

    hbm, vmem = pl.BlockSpec(memory_space=pl.ANY), pl.BlockSpec(memory_space=pltpu.VMEM)
    return pl.pallas_call(
        body,
        out_shape=jax.ShapeDtypeStruct(s_half.shape, F32),
        in_specs=[hbm, hbm, hbm, vmem],
        out_specs=vmem,
        scratch_shapes=[*bufs.values(), *sems.values()],
        compiler_params=pltpu.CompilerParams(
            collective_id=0, has_side_effects=True, vmem_limit_bytes=60 << 20
        ),
        name="gw_update",
    )(sigma_m, sigma_n, coeffs, s_half)


def solution(mesh):
    in_specs = (P("bulk", "col"),) * 3 + (P(("bulk", "col"), None),)
    return jax.shard_map(
        shards,
        mesh=mesh,
        in_specs=in_specs,
        out_specs=P(("bulk", "col"), None),
        check_vma=False,
    )
```
